128 devices in a mesh: section: 4 (over y), dp: 2 (over core), expert: 16 (over x, z).
Axes of the slice: x: 4, y: 4, z: 4, core: 2. Of those that a mesh axis runs over, the one named last changes fastest.
Arguments:
- stashed: bfloat16 [4, 6144, 2048], P('section', ('dp', 'expert')), may hold values from -6 to 6
- expert_ids: int32 [4, 6144, 8], P('section', ('dp', 'expert')), may hold values from 0 to 63, all different within a row; in each aligned block of 192 rows (0 to 191, 192 to 383, ..., all dimensions but the last counted through in order) at most 48 rows name the same one
- route_probs: float32 [4, 6144, 8], P('section', ('dp', 'expert')), may hold values from 0.02 to 1
- w_gate: bfloat16 [4, 64, 2048, 768], P('section', ('dp', 'expert')), may hold values from -0.125 to 0.125
- w_up: bfloat16 [4, 64, 2048, 768], P('section', ('dp', 'expert')), may hold values from -0.125 to 0.125
- w_down: bfloat16 [4, 64, 768, 2048], P('section', ('dp', 'expert')), may hold values from -0.21875 to 0.21875
Outputs:
- handed: bfloat16 [4, 6144, 2048], P('section', ('dp', 'expert'))
- balance: float32 [4], P('section')
The draws below stay inside these ranges and needn't reach their ends.
Inputs may be any that keep to these rules, and one draw needn't show every extreme that they name: `expert_ids`: each token names 8 different experts; among the tokens of one device (aligned blocks of 192 tokens) no expert is named more than 48 times, and in every draw some expert is named exactly 48 times in some block.
All inputs are finite; a program needn't handle non-finite values.
Results may differ from the reference program's by a relative error of at most 0.0032.
Values may be sent and summed in bfloat16 or wider, within the bound.
No kernel may reach another device: no remote copies, remote signals or barrier semaphores. Data moves between devices by JAX's collectives and lax.ppermute only.
A program may use at most 128 MiB of HBM per device.

```python
import math
import jax
import jax.numpy as jnp
import numpy as np
from jax import lax

D = 2048
FF = 768
TOPK = 8
TOK_DEV = 192
SECTIONS = 4
TOKENS = 6144
EXPERTS = 64
CAP = 48


def block_scale(stream_key, dims, split, low, largest):
    def one(dim, parts):
        heights = jax.random.uniform(jax.random.fold_in(jax.random.fold_in(stream_key, 6), dim), (parts,), jnp.float32, low / len(split), largest / len(split))
        return jnp.repeat(jnp.exp(heights), dims[dim] // parts).reshape((-1,) + (1,) * (len(dims) - dim - 1))

    factor_of = one(*split[0])
    for cut in split[1:]:
        factor_of = factor_of * one(*cut)
    return factor_of


def assign_block(rng, own, number, rows, number_of, top, most, skew):
    ranking = jax.random.permutation(rng, number_of)
    heavy_load, ordinary = portions_of(number_of, rows * top, most, skew, True), portions_of(number_of, rows * top, most, skew, False)
    places = jnp.arange(number_of)

    def named(lengths, turn):
        used = int((lengths > 0).sum())
        fixed = max(1, used // 4)
        passed = fixed + (places - fixed + turn * (used - fixed)) % max(1, number_of - fixed)
        return jnp.zeros((number_of,), jnp.int32).at[ranking[jnp.where(places < fixed, places, passed)]].set(jnp.asarray(lengths, jnp.int32))

    lengths = jnp.where(number % 4 == 0, named(heavy_load, number // 4), named(ordinary, number - number // 4 - 1))
    mixed = jax.random.permutation(jax.random.fold_in(own, 3), number_of)
    donor, sink = mixed[0:number_of // 2 * 2:2], mixed[1:number_of // 2 * 2:2]
    slack = jnp.minimum(lengths[donor] - 1, most - lengths[sink]) // 2
    slack = jnp.where((donor == ranking[0]) | (sink == ranking[0]) | (lengths[sink] == 0), 0, jnp.maximum(slack, 0))
    passed = jax.random.randint(jax.random.fold_in(own, 4), (number_of // 2,), 0, 1 << 20) % (slack + 1)
    lengths = lengths.at[donor].add(-passed).at[sink].add(passed)
    members = jnp.searchsorted(jnp.cumsum(lengths), jnp.arange(rows * top), side="right").astype(jnp.int32)
    grid = members.reshape(top, rows).T
    grid = grid[jax.random.permutation(jax.random.fold_in(own, 1), rows)]
    turn = jax.random.randint(jax.random.fold_in(own, 2), (rows, 1), 0, top)
    return jnp.take_along_axis(grid, (jnp.arange(top)[None, :] + turn) % top, axis=1)


def portions_of(number_of, total, limit, skew, full):
    portions = [(1 << 20) // math.isqrt(standing ** skew) + 1 for standing in range(1, number_of + 1)]
    largest = limit if full else min(limit, max(-(-total // number_of), total * portions[0] // sum(portions)))
    least = 1 if total - largest >= number_of - 1 else 0
    given, spare = [largest] + [least] * (number_of - 1), total - largest - least * (number_of - 1)
    while spare > 0:
        candidates = [i for i in range(1, number_of) if given[i] < largest] or [i for i in range(1, number_of) if given[i] < limit]
        whole, budget = sum([portions[i] for i in candidates]), spare
        for i in candidates:
            more = min(limit - given[i], max(1, budget * portions[i] // whole), spare)
            given[i] = given[i] + more
            spare = spare - more
    return np.array(given)


def centred(stream_key, shape, spread, bound, split=(), kind=jnp.bfloat16):
    drawn = jax.random.normal(stream_key, shape, jnp.float32) * spread
    if len(split) > 0:
        drawn = block_scale(stream_key, shape, split, -0.22, 0.18) * drawn
    return jnp.clip(drawn, min=-bound, max=bound).astype(kind)


def setup_inputs(seed: int = 0) -> dict:
    streams_of = jax.random.split(jax.random.key(seed), 7)
    stashed = centred(streams_of[0], (SECTIONS, TOKENS, D), 1.0, 6.0, ((0, 4), (1, 32)))
    expert_ids_keys = jax.random.split(jax.random.fold_in(streams_of[1], 1), SECTIONS * TOKENS // TOK_DEV)
    expert_ids_turns = jax.random.permutation(jax.random.fold_in(streams_of[1], 3), SECTIONS * TOKENS // TOK_DEV)
    expert_ids = jax.vmap(lambda own, number: assign_block(jax.random.fold_in(streams_of[1], 2), own, number, TOK_DEV, EXPERTS, TOPK, CAP, 2))(expert_ids_keys, expert_ids_turns).reshape((SECTIONS, TOKENS, TOPK))
    route_probs = jnp.clip(jnp.exp(math.log(1.0) - 3.912023 * jax.random.uniform(streams_of[2], (SECTIONS, TOKENS, TOPK), jnp.float32) ** block_scale(streams_of[2], (SECTIONS, TOKENS, TOPK), ((0, 4), (1, 32)), -0.2, 0.2)), 0.02, 1.0)
    w_gate = centred(streams_of[3], (SECTIONS, EXPERTS, D, FF), D ** -0.5, 0.125, ((0, 4), (1, 32)))
    w_up = centred(streams_of[4], (SECTIONS, EXPERTS, D, FF), D ** -0.5, 0.125, ((0, 4), (1, 32)))
    w_down = centred(streams_of[5], (SECTIONS, EXPERTS, FF, D), FF ** -0.5, 0.21875, ((0, 4), (1, 32)))
    return {"stashed": stashed, "expert_ids": expert_ids, "route_probs": route_probs, "w_gate": w_gate, "w_up": w_up, "w_down": w_down}


def expert_ffn(rows, gate_w, up_w, down_w):
    gate_act = jnp.dot(rows, gate_w, preferred_element_type=jnp.float32)
    up_act = jnp.dot(rows, up_w, preferred_element_type=jnp.float32)
    hidden = (jax.nn.silu(gate_act) * up_act).astype(jnp.bfloat16)
    return jnp.dot(hidden, down_w, preferred_element_type=jnp.float32).astype(jnp.bfloat16)

def moe_layer(tokens_in, choice_ids, probs, gate_w, up_w, down_w):
    blocks = TOKENS // TOK_DEV
    inputs = tokens_in.astype(jnp.float32)
    normed = (inputs * lax.rsqrt(lax.optimization_barrier(jnp.mean(inputs * inputs, axis=-1, keepdims=True)) + 1e-06)).astype(jnp.bfloat16)
    normed_pad = jnp.concatenate([normed, jnp.zeros((1, D), jnp.bfloat16)], axis=0)
    grouped = choice_ids.reshape(blocks, TOK_DEV * TOPK)
    labels = jnp.arange(EXPERTS, dtype=jnp.int32)
    onehot = (grouped[:, :, None] == labels[None, None, :]).astype(jnp.int32)
    running = jnp.cumsum(onehot, axis=1).astype(jnp.int32)
    position = (lax.optimization_barrier(jnp.sum(running * onehot, axis=2)).astype(jnp.int32) - 1).reshape(TOKENS, TOPK)
    block_index = (jnp.arange(TOKENS, dtype=jnp.int32) // TOK_DEV)[:, None]
    slot_rows = (block_index * CAP + position).astype(jnp.int32)
    weights = probs / lax.optimization_barrier(jnp.sum(probs, axis=-1, keepdims=True))
    token_index = jnp.broadcast_to(jnp.arange(TOKENS, dtype=jnp.int32)[:, None], (TOKENS, TOPK)).astype(jnp.int32)
    slot_token = jnp.full((EXPERTS, blocks * CAP), TOKENS, jnp.int32).at[choice_ids, slot_rows].set(token_index)
    slot_weight = jnp.zeros((EXPERTS, blocks * CAP), weights.dtype).at[choice_ids, slot_rows].set(weights)

    def one_expert(mixture, packed):
        rows_idx, row_w, g_w, u_w, d_w = packed
        rows = normed_pad[rows_idx]
        out = expert_ffn(rows, g_w, u_w, d_w).astype(mixture.dtype)
        return (mixture.at[rows_idx].add(row_w[:, None].astype(mixture.dtype) * out), None)
    start = jnp.zeros((TOKENS + 1, D), inputs.dtype)
    mixture, unused = lax.scan(one_expert, start, (slot_token, slot_weight, gate_w, up_w, down_w))
    layer_out = (inputs + mixture[:TOKENS]).astype(jnp.bfloat16)
    counts = lax.optimization_barrier(jnp.sum(onehot, axis=(0, 1))).astype(weights.dtype)
    flat_hot = onehot.reshape(TOKENS * TOPK, EXPERTS).astype(weights.dtype)
    mass = jnp.dot(weights.reshape(-1), flat_hot, precision=lax.Precision.HIGHEST)
    loss = EXPERTS * jnp.sum(counts / (TOKENS * TOPK) * (mass / TOKENS))
    return (layer_out, loss)

def reference(stashed, expert_ids, route_probs, w_gate, w_up, w_down):
    layers = []
    losses = []
    for section_index in range(SECTIONS):
        layer_out, loss = moe_layer(stashed[section_index], expert_ids[section_index], route_probs[section_index], w_gate[section_index], w_up[section_index], w_down[section_index])
        layers.append(layer_out)
        losses.append(loss)
    stacked = jnp.stack(layers)
    handed = jnp.concatenate([stacked[-1:], stacked[:-1]], axis=0)
    return (handed, jnp.stack(losses).astype(jnp.float32))
```

```python
import jax
import jax.numpy as jnp
from jax import lax
from jax.experimental import pallas as pl
from jax.experimental.pallas import tpu as pltpu
from jax.sharding import PartitionSpec as P

SIDE = 4
STEPS = (0, -1, 1, 2)
TILE = 256
ALIGN = 16


def plane_pairs(step_x, step_z):
    pairs = []
    for x in range(SIDE):
        for z in range(SIDE):
            goal = ((x + step_x) % SIDE) * SIDE + (z + step_z) % SIDE
            pairs.append((x * SIDE + z, goal))
    return pairs


def along_x(value, step):
    return lax.ppermute(value, "expert", plane_pairs(step, 0))


def along_z(value, step):
    return lax.ppermute(value, "expert", plane_pairs(0, step))


def gather_ring(value, send):
    half = value.shape[0] // 2
    low = send(value, 1)
    high = send(value, -1)
    far_a = send(low[:half], 1)
    far_b = send(high[half:], -1)
    return value, low, high, far_a, far_b


def reduce_ring(own, low, high, far_a, far_b, send):
    half = far_a.shape[0]
    from_low = send(far_a, 1)
    from_high = send(far_b, -1)
    to_high = jnp.concatenate([high[:half] + from_low, high[half:]])
    to_low = jnp.concatenate([low[:half], low[half:] + from_high])
    a = send(to_high, 1)
    b = send(to_low, -1)
    return own.astype(jnp.float32) + a.astype(jnp.float32) + b.astype(jnp.float32)


def expert_kernel(tokens, experts, cap, width, hidden):
    blocks = SIDE * SIDE
    half = tokens // 2
    slots = experts * cap
    rows = blocks * cap

    def body(
        count_ref, source_ref, meta_ref,
        a0, a1, a2, a3, a4, b0, b1, b2, b3, b4,
        gate_own, up_own, down_own, gate_far, up_far, down_far,
        oa0, oa1, oa2, oa3, oa4, ob0, ob1, ob2, ob3, ob4,
        tok, packed, scale, gate_buf, up_buf, down_buf, offsets,
        in_sem, w_sem, out_sem,
    ):
        def piece(refs, major, minor):
            if major < 3:
                return refs[major].at[pl.ds(minor * half, half)]
            return refs[3 + minor // 2].at[pl.ds((minor % 2) * half, half)]

        ins_a, ins_b = (a0, a1, a2, a3, a4), (b0, b1, b2, b3, b4)
        outs_a, outs_b = (oa0, oa1, oa2, oa3, oa4), (ob0, ob1, ob2, ob3, ob4)

        def in_copies(block):
            dx, dz = block // SIDE, block % SIDE
            return (
                pltpu.make_async_copy(piece(ins_a, dz, dx), tok.at[block, pl.ds(0, half)], in_sem.at[block, 0]),
                pltpu.make_async_copy(piece(ins_b, dx, dz), tok.at[block, pl.ds(half, half)], in_sem.at[block, 1]),
            )

        def out_copies(block):
            dx, dz = block // SIDE, block % SIDE
            return (
                pltpu.make_async_copy(tok.at[block, pl.ds(0, half)], piece(outs_a, dz, dx), out_sem.at[block, 0]),
                pltpu.make_async_copy(tok.at[block, pl.ds(half, half)], piece(outs_b, dx, dz), out_sem.at[block, 1]),
            )

        def weight_copies(e):
            group = (gate_own, up_own, down_own) if e < 2 else (gate_far, up_far, down_far)
            return [
                pltpu.make_async_copy(src.at[e % 2], dst.at[e % 2], w_sem.at[e, i])
                for i, (src, dst) in enumerate(zip(group, (gate_buf, up_buf, down_buf)))
            ]

        for block in range(blocks):
            for copy in in_copies(block):
                copy.start()
        for e in range(2):
            for copy in weight_copies(e):
                copy.start()

        for e in range(experts):
            offset = jnp.int32(0)
            for block in range(blocks):
                offsets[e, block] = offset
                count = count_ref[source_ref[block], e]
                offset = offset + (count + ALIGN - 1) // ALIGN * ALIGN
            offsets[e, blocks] = offset

        slot_index = lax.broadcasted_iota(jnp.int32, (cap, tokens), 0).astype(jnp.float32)

        def hot(block, e):
            return slot_index == meta_ref[source_ref[block], pl.ds(e, 1), pl.ds(0, tokens)]

        for block in range(blocks):
            for copy in in_copies(block):
                copy.wait()
            masks = [hot(block, e) for e in range(experts)]
            select = jnp.concatenate([m.astype(jnp.float32) for m in masks]).astype(jnp.bfloat16)
            taken = jnp.dot(select, tok[block], preferred_element_type=jnp.float32).astype(jnp.bfloat16)
            for e in range(experts):
                start = pl.multiple_of(offsets[e, block], ALIGN)
                packed[e, pl.ds(start, cap), :] = taken[e * cap : (e + 1) * cap]
                share = meta_ref[source_ref[block], pl.ds(experts + e, 1), pl.ds(0, tokens)]
                summed = jnp.sum(jnp.where(masks[e], share, 0.0), axis=1, keepdims=True)
                scale[e, pl.ds(start, cap), :] = jnp.broadcast_to(summed, (cap, 128))

        for e in range(experts):
            for copy in weight_copies(e):
                copy.wait()

            def tile_step(t, carry):
                window = pl.ds(pl.multiple_of(t * TILE, TILE), TILE)
                inputs = packed[e, window, :]
                gate = jnp.dot(inputs, gate_buf[e % 2], preferred_element_type=jnp.float32)
                up = jnp.dot(inputs, up_buf[e % 2], preferred_element_type=jnp.float32)
                act = (gate * jax.nn.sigmoid(gate) * up).astype(jnp.bfloat16)
                out = jnp.dot(act, down_buf[e % 2], preferred_element_type=jnp.float32)
                packed[e, window, :] = (out * scale[e, window, 0:1]).astype(jnp.bfloat16)
                return carry

            lax.fori_loop(0, (offsets[e, blocks] + TILE - 1) // TILE, tile_step, 0)
            if e + 2 < experts:
                for copy in weight_copies(e + 2):
                    copy.start()

        for block in range(blocks):
            select = jnp.concatenate(
                [hot(block, e).astype(jnp.float32) for e in range(experts)]
            ).astype(jnp.bfloat16)
            results = jnp.concatenate(
                [packed[e, pl.ds(pl.multiple_of(offsets[e, block], ALIGN), cap), :] for e in range(experts)]
            )
            total = lax.dot_general(
                select, results, (((0,), (0,)), ((), ())), preferred_element_type=jnp.float32
            )
            tok[block] = total.astype(jnp.bfloat16)
            for copy in out_copies(block):
                copy.start()
        for block in range(blocks):
            for copy in out_copies(block):
                copy.wait()

    any_spec = pl.BlockSpec(memory_space=pl.ANY)
    smem = pl.BlockSpec(memory_space=pltpu.SMEM)
    full = jax.ShapeDtypeStruct((SIDE * half, width), jnp.bfloat16)
    part = jax.ShapeDtypeStruct((SIDE * half // 2, width), jnp.bfloat16)
    return pl.pallas_call(
        body,
        in_specs=[smem, smem, pl.BlockSpec(memory_space=pltpu.VMEM)] + [any_spec] * 16,
        out_specs=[any_spec] * 10,
        out_shape=[full, full, full, part, part] * 2,
        scratch_shapes=[
            pltpu.VMEM((blocks, tokens, width), jnp.bfloat16),
            pltpu.VMEM((experts, rows, width), jnp.bfloat16),
            pltpu.VMEM((experts, rows, 128), jnp.float32),
            pltpu.VMEM((2, width, hidden), jnp.bfloat16),
            pltpu.VMEM((2, width, hidden), jnp.bfloat16),
            pltpu.VMEM((2, hidden, width), jnp.bfloat16),
            pltpu.SMEM((experts, blocks + 1), jnp.int32),
            pltpu.SemaphoreType.DMA((blocks, 2)),
            pltpu.SemaphoreType.DMA((experts, 3)),
            pltpu.SemaphoreType.DMA((blocks, 2)),
        ],
        compiler_params=pltpu.CompilerParams(vmem_limit_bytes=60 * 1024 * 1024),
        name="experts",
    )


def swapped(value):
    return lax.ppermute(value, "dp", [(0, 1), (1, 0)])


def per_device(stashed, expert_ids, route_probs, w_gate, w_up, w_down):
    tokens_in = stashed[0]
    choice_ids = expert_ids[0]
    probs = route_probs[0]
    chips = lax.axis_size("expert")
    local_count = w_gate.shape[1]
    experts = 2 * local_count
    all_experts = chips * experts
    token_count, top_count = choice_ids.shape
    width = tokens_in.shape[1]
    hidden = w_gate.shape[3]
    cap = 2 * token_count * top_count // all_experts
    half = token_count // 2

    inputs = tokens_in.astype(jnp.float32)
    normed = (inputs * lax.rsqrt(jnp.mean(inputs * inputs, axis=-1, keepdims=True) + 1e-06)).astype(
        jnp.bfloat16
    )
    a_ring = gather_ring(normed[:half], along_x)
    b_ring = gather_ring(normed[half:], along_z)
    a_parts = gather_ring(jnp.concatenate(a_ring), along_z)
    b_parts = gather_ring(jnp.concatenate(b_ring), along_x)
    far = [swapped(w[0]) for w in (w_gate, w_up, w_down)]

    place = lax.axis_index("expert")
    side = lax.axis_index("dp")
    weights = probs / jnp.sum(probs, axis=-1, keepdims=True)
    ids_t = choice_ids.T
    weights_t = weights.T
    member = jnp.arange(experts, dtype=jnp.int32)
    owner = jnp.where(member < local_count, side, 1 - side)
    labels = (
        owner[None, :] * (all_experts // 2)
        + jnp.arange(chips, dtype=jnp.int32)[:, None] * local_count
        + (member % local_count)[None, :]
    ).reshape(-1)
    match = ids_t[None, :, :] == labels[:, None, None]
    chosen = jnp.any(match, axis=1)
    share = jnp.sum(jnp.where(match, weights_t[None], 0.0), axis=1)
    order = jnp.arange(token_count, dtype=jnp.int32)
    earlier = (order[:, None] < order[None, :]).astype(jnp.bfloat16)
    before = jnp.dot(chosen.astype(jnp.bfloat16), earlier, preferred_element_type=jnp.float32)
    position = jnp.where(chosen, before, -1.0)
    tallies = jnp.stack([jnp.sum(chosen.astype(jnp.float32), axis=1), jnp.sum(share, axis=1)])
    dense = jnp.concatenate(
        [position.reshape(chips, experts, token_count), share.reshape(chips, experts, token_count)], axis=1
    )
    extra = jnp.concatenate([tallies, jnp.zeros((2 * experts - 2, all_experts), jnp.float32)])
    extra = jnp.broadcast_to(extra[None], (chips,) + extra.shape)
    meta = lax.all_to_all(
        jnp.concatenate([dense, extra], axis=2), "expert", split_axis=0, concat_axis=0, tiled=True
    )
    counts = (jnp.max(meta[:, :experts, :token_count], axis=2) + 1.0).astype(jnp.int32)
    sums = jnp.sum(meta[:, :2, token_count:], axis=0)
    other = swapped(sums).reshape(2, chips, 2, local_count)[:, :, ::-1].reshape(2, all_experts)
    sums = sums + other
    tokens_all = token_count * 2 * chips
    loss = all_experts * jnp.sum(sums[0] / (tokens_all * top_count) * (sums[1] / tokens_all))

    x, z = place // SIDE, place % SIDE
    step = jnp.array(STEPS, jnp.int32)
    source = (((x + step) % SIDE)[:, None] * SIDE + ((z + step) % SIDE)[None, :]).reshape(-1)

    run = expert_kernel(token_count, experts, cap, width, hidden)
    outs = run(counts, source, meta, *a_parts, *b_parts, w_gate[0], w_up[0], w_down[0], *far)

    a_line = reduce_ring(*outs[:5], along_z).astype(jnp.bfloat16)
    b_line = reduce_ring(*outs[5:], along_x).astype(jnp.bfloat16)

    def finish(line, send, lo):
        cut = half
        own, low, high = (line[i * cut : (i + 1) * cut] for i in range(3))
        far_a, far_b = line[3 * cut : 3 * cut + cut // 2], line[3 * cut + cut // 2 :]
        mixed = reduce_ring(own, low, high, far_a, far_b, send)
        out = (inputs[lo : lo + half] + mixed).astype(jnp.bfloat16)
        count = lax.axis_size("section")
        return lax.ppermute(out, "section", [(s, (s + 1) % count) for s in range(count)])

    handed = jnp.concatenate([finish(a_line, along_x, 0), finish(b_line, along_z, half)])
    return (handed[None], loss.reshape(1))


def solution(mesh):
    placed = (
        P("section", ("dp", "expert"), None),
        P("section", ("dp", "expert"), None),
        P("section", ("dp", "expert"), None),
        P("section", ("dp", "expert"), None, None),
        P("section", ("dp", "expert"), None, None),
        P("section", ("dp", "expert"), None, None),
    )
    return jax.shard_map(
        per_device,
        mesh=mesh,
        in_specs=placed,
        out_specs=(P("section", ("dp", "expert"), None), P("section")),
        check_vma=False,
    )
```

```python
import jax
import jax.numpy as jnp
from jax import lax
from jax.experimental import pallas as pl
from jax.experimental.pallas import tpu as pltpu
from jax.sharding import PartitionSpec as P


SIDE = 4
STEPS = (0, -1, 1, 2)
TILE = 256
ALIGN = 16
FAR = 3
GROUP = 4


def plane_pairs(step_x, step_z):
    pairs = []
    for x in range(SIDE):
        for z in range(SIDE):
            goal = ((x + step_x) % SIDE) * SIDE + (z + step_z) % SIDE
            pairs.append((x * SIDE + z, goal))
    return pairs


def along_x(value, step):
    return lax.ppermute(value, "expert", plane_pairs(step, 0))


def along_z(value, step):
    return lax.ppermute(value, "expert", plane_pairs(0, step))


def gather_plane(own, first, second):
    half = own.shape[0] // 2
    low, high = first(own, 1), first(own, -1)
    low_own, high_own = second(own, 1), second(own, -1)
    far = jnp.concatenate([first(low[:half], 1), first(high[half:], -1)])
    pair = jnp.concatenate([low, high])
    low_pair, high_pair = second(pair, 1), second(pair, -1)
    far_own = second(low_own, 1)
    low_far, high_far = second(far, 1), second(far, -1)
    far_pair = second(high_pair, -1)
    far_far = second(low_far, 1)
    near = [own, pair, far, low_own, low_pair, low_far, high_own, high_pair, high_far]
    return near, [far_own, far_pair, far_far]


def reduce_line(plus, minus, high, low, own, send):
    cut = high.shape[0]
    from_low, from_high = send(plus, 1), send(minus, -1)
    last_low = send(high + from_low[:cut], 1)
    last_high = send(low + from_high[:cut], -1)
    wide = lambda v: v.astype(jnp.float32)
    return jnp.concatenate(
        [
            wide(own[:cut]) + wide(from_high[cut:]) + wide(last_low),
            wide(own[cut:]) + wide(from_low[cut:]) + wide(last_high),
        ]
    )


def out_segments(step, start, size, cut):
    segments = []
    for lo, hi in ((start, min(start + size, cut)), (max(start, cut), start + size)):
        if hi <= lo:
            continue
        early = lo < cut
        if step == 0:
            segments.append((4, lo, lo - start, hi - lo))
        elif step == FAR:
            segments.append((0 if early else 1, lo if early else lo - cut, lo - start, hi - lo))
        elif step == 2:
            segments.append((2 if early else 0, lo, lo - start, hi - lo))
        else:
            segments.append((1 if early else 3, lo + cut if early else lo - cut, lo - start, hi - lo))
    return segments


def expert_kernel(near, tokens, experts, cap, width, hidden):
    half = tokens // 2
    held = (0, 1, 2) if near else (FAR,)
    lines = len(held)
    units = []
    for dx in range(SIDE):
        for dz in range(SIDE):
            has_a, has_b = dz in held, dx in held
            if has_a or has_b:
                units.append((dx, dz, has_a, has_b))
    n_units = len(units)
    rows = -(-(n_units * cap) // TILE) * TILE
    n_in = 3 * lines

    def body(*refs):
        count_ref, first_ref, source_ref, meta_ref = refs[:4]
        ins = (refs[4 : 4 + n_in], refs[4 + n_in : 4 + 2 * n_in])
        at = 4 + 2 * n_in
        own_w, far_w = refs[at : at + 3], refs[at + 3 : at + 6]
        outs = (refs[at + 6 : at + 11], refs[at + 11 : at + 16])
        (tok, packed, scale, gate_buf, up_buf, down_buf, offsets, limits, in_sem, w_sem, out_sem) = refs[at + 16 :]
        bufs = (gate_buf, up_buf, down_buf)

        def in_copies(u):
            dx, dz, has_a, has_b = units[u]
            copies = []
            for side, (has, line, inner) in enumerate(((has_a, dz, dx), (has_b, dx, dz))):
                if has:
                    group = ins[side][3 * held.index(line) : 3 * held.index(line) + 3]
                    src = (group[0], group[1].at[pl.ds(0, half)], group[1].at[pl.ds(half, half)], group[2])[inner]
                    copies.append(
                        pltpu.make_async_copy(src, tok.at[u, pl.ds(side * half, half)], in_sem.at[u, side])
                    )
            return copies

        def out_copies(u):
            dx, dz, has_a, has_b = units[u]
            copies = []
            for side, (has, line, inner) in enumerate(((has_a, dz, dx), (has_b, dx, dz))):
                if has:
                    parts = out_segments(inner, held.index(line) * half, half, lines * half // 2)
                    for i, (which, row, offset, size) in enumerate(parts):
                        copies.append(
                            pltpu.make_async_copy(
                                tok.at[u, pl.ds(side * half + offset, size)],
                                outs[side][which].at[pl.ds(row, size)],
                                out_sem.at[u, 2 * side + i],
                            )
                        )
            return copies

        def weight_copies(e, group):
            return [
                pltpu.make_async_copy(src.at[e % 2], dst.at[e % 2], w_sem.at[e % 2, i])
                for i, (src, dst) in enumerate(zip(group, bufs))
            ]

        for u in range(n_units):
            for copy in in_copies(u):
                copy.start()
        for e in range(2):
            for copy in weight_copies(e, own_w):
                copy.start()

        for e in range(experts):
            offset = jnp.int32(0)
            for u, (dx, dz, has_a, has_b) in enumerate(units):
                offsets[e, u] = offset
                spot = source_ref[dx * SIDE + dz]
                count, first = count_ref[spot, e], first_ref[spot, e]
                size = count if has_a and has_b else (first if has_a else count - first)
                offset = offset + (size + ALIGN - 1) // ALIGN * ALIGN
            offsets[e, n_units] = offset

        for u, (dx, dz, has_a, has_b) in enumerate(units):
            limits[0, u] = source_ref[dx * SIDE + dz]
            limits[1, u] = jnp.int32(0 if has_a else half)
            limits[2, u] = jnp.int32(tokens if has_b else half)
            limits[3, u] = jnp.int32(0 if has_a else 1)

        slot_index = lax.broadcasted_iota(jnp.int32, (cap, tokens), 0)
        lane = lax.broadcasted_iota(jnp.int32, (1, tokens), 1)

        def masks_of(u):
            spot = limits[0, u]
            inside = (lane >= limits[1, u]) & (lane < limits[2, u])
            masks = []
            for e in range(experts):
                place = meta_ref[spot, pl.ds(e, 1), pl.ds(0, tokens)].astype(jnp.int32)
                place = jnp.where(inside, place - limits[3, u] * first_ref[spot, e], -1)
                masks.append(slot_index == place)
            return masks

        def as_matrix(masks):
            return jnp.concatenate([m.astype(jnp.float32) for m in masks]).astype(jnp.bfloat16)

        groups = [range(i, min(i + GROUP, n_units)) for i in range(0, n_units, GROUP)]

        def pack_step(u, carry):
            masks = masks_of(u)
            taken = jnp.dot(as_matrix(masks), tok[u], preferred_element_type=jnp.float32).astype(jnp.bfloat16)
            for e in range(experts):
                start = pl.multiple_of(offsets[e, u], ALIGN)
                packed[e, pl.ds(start, cap), :] = taken[e * cap : (e + 1) * cap]
                share = meta_ref[limits[0, u], pl.ds(experts + e, 1), pl.ds(0, tokens)]
                summed = jnp.sum(jnp.where(masks[e], share, 0.0), axis=1, keepdims=True)
                scale[e, pl.ds(start, cap), :] = jnp.broadcast_to(summed, (cap, 128))
            return carry

        def blank_step(u, carry):
            @pl.when(limits[1, u] > 0)
            def _():
                tok[u, pl.ds(0, half), :] = jnp.zeros((half, width), jnp.bfloat16)

            @pl.when(limits[2, u] < tokens)
            def _():
                tok[u, pl.ds(half, half), :] = jnp.zeros((half, width), jnp.bfloat16)

            return carry

        lax.fori_loop(0, n_units, blank_step, 0)
        for group in groups:
            for u in group:
                for copy in in_copies(u):
                    copy.wait()
            lax.fori_loop(group[0], group[-1] + 1, pack_step, 0)

        def expert_step(e, carry):
            slot = e % 2
            for copy in weight_copies(e, own_w):
                copy.wait()

            def rows_step(start, size):
                window = pl.ds(pl.multiple_of(start, size), size)
                inputs = packed[e, window, :]
                gate = jnp.dot(inputs, gate_buf[slot], preferred_element_type=jnp.float32)
                up = jnp.dot(inputs, up_buf[slot], preferred_element_type=jnp.float32)
                act = (gate * jax.nn.sigmoid(gate) * up).astype(jnp.bfloat16)
                out = jnp.dot(act, down_buf[slot], preferred_element_type=jnp.float32)
                packed[e, window, :] = (out * scale[e, window, 0:1]).astype(jnp.bfloat16)

            total = offsets[e, n_units]
            short = TILE // 2
            n_full = (total + short - 1) // TILE

            def tile_step(t, inner):
                rows_step(t * TILE, TILE)
                return inner

            lax.fori_loop(0, n_full, tile_step, 0)

            @pl.when(n_full * TILE < total)
            def _():
                rows_step(n_full * TILE, short)

            @pl.when(e < experts - 2)
            def _():
                for copy in weight_copies(e, far_w):
                    copy.start()

            return carry

        lax.fori_loop(0, experts, expert_step, 0)

        def join_step(u, carry):
            results = jnp.concatenate(
                [packed[e, pl.ds(pl.multiple_of(offsets[e, u], ALIGN), cap), :] for e in range(experts)]
            )
            total = lax.dot_general(
                as_matrix(masks_of(u)), results, (((0,), (0,)), ((), ())), preferred_element_type=jnp.float32
            )
            tok[u] = total.astype(jnp.bfloat16)
            return carry

        for group in groups:
            lax.fori_loop(group[0], group[-1] + 1, join_step, 0)
            for u in group:
                for copy in out_copies(u):
                    copy.start()
        for u in range(n_units):
            for copy in out_copies(u):
                copy.wait()

    any_spec = pl.BlockSpec(memory_space=pl.ANY)
    smem = pl.BlockSpec(memory_space=pltpu.SMEM)
    line = lines * half
    shapes = [jax.ShapeDtypeStruct((n, width), jnp.bfloat16) for n in (line, line, line // 2, line // 2, line)]
    return pl.pallas_call(
        body,
        in_specs=[smem, smem, smem, pl.BlockSpec(memory_space=pltpu.VMEM)] + [any_spec] * (2 * n_in + 6),
        out_specs=[any_spec] * 10,
        out_shape=shapes * 2,
        scratch_shapes=[
            pltpu.VMEM((n_units, tokens, width), jnp.bfloat16),
            pltpu.VMEM((experts, rows, width), jnp.bfloat16),
            pltpu.VMEM((experts, rows, 128), jnp.float32),
            pltpu.VMEM((2, width, hidden), jnp.bfloat16),
            pltpu.VMEM((2, width, hidden), jnp.bfloat16),
            pltpu.VMEM((2, hidden, width), jnp.bfloat16),
            pltpu.SMEM((experts, n_units + 1), jnp.int32),
            pltpu.SMEM((4, n_units), jnp.int32),
            pltpu.SemaphoreType.DMA((n_units, 2)),
            pltpu.SemaphoreType.DMA((2, 3)),
            pltpu.SemaphoreType.DMA((n_units, 4)),
        ],
        compiler_params=pltpu.CompilerParams(vmem_limit_bytes=56 * 1024 * 1024),
        name="experts_near" if near else "experts_far",
    )


def swapped(value):
    return lax.ppermute(value, "dp", [(0, 1), (1, 0)])


def layer(stashed, expert_ids, route_probs, w_gate, w_up, w_down):
    tokens_in = stashed[0]
    choice_ids = expert_ids[0]
    probs = route_probs[0]
    chips = lax.axis_size("expert")
    local_count = w_gate.shape[1]
    experts = 2 * local_count
    all_experts = chips * experts
    token_count, top_count = choice_ids.shape
    width = tokens_in.shape[1]
    hidden = w_gate.shape[3]
    cap = 2 * token_count * top_count // all_experts
    half = token_count // 2

    inputs = tokens_in.astype(jnp.float32)
    normed = (inputs * lax.rsqrt(jnp.mean(inputs * inputs, axis=-1, keepdims=True) + 1e-06)).astype(
        jnp.bfloat16
    )
    a_near, a_far = gather_plane(normed[:half], along_x, along_z)
    b_near, b_far = gather_plane(normed[half:], along_z, along_x)
    far_w = [swapped(w[0]) for w in (w_gate, w_up, w_down)]
    own_w = [w[0] for w in (w_gate, w_up, w_down)]

    place = lax.axis_index("expert")
    side = lax.axis_index("dp")
    weights = probs / jnp.sum(probs, axis=-1, keepdims=True)
    ids_t = choice_ids.T
    weights_t = weights.T
    member = jnp.arange(experts, dtype=jnp.int32)
    owner = jnp.where(member < local_count, side, 1 - side)
    labels = (
        owner[None, :] * (all_experts // 2)
        + jnp.arange(chips, dtype=jnp.int32)[:, None] * local_count
        + (member % local_count)[None, :]
    ).reshape(-1)
    match = ids_t[None, :, :] == labels[:, None, None]
    chosen = jnp.any(match, axis=1)
    share = jnp.sum(jnp.where(match, weights_t[None], 0.0), axis=1)
    order = jnp.arange(token_count, dtype=jnp.int32)
    earlier = (order[:, None] < order[None, :]).astype(jnp.bfloat16)
    before = jnp.dot(chosen.astype(jnp.bfloat16), earlier, preferred_element_type=jnp.float32)
    position = jnp.where(chosen, before, -1.0)
    tallies = jnp.stack([jnp.sum(chosen.astype(jnp.float32), axis=1), jnp.sum(share, axis=1)])
    dense = jnp.concatenate(
        [position.reshape(chips, experts, token_count), share.reshape(chips, experts, token_count)], axis=1
    )
    extra = jnp.concatenate([tallies, jnp.zeros((2 * experts - 2, all_experts), jnp.float32)])
    extra = jnp.broadcast_to(extra[None], (chips,) + extra.shape)
    meta = lax.all_to_all(
        jnp.concatenate([dense, extra], axis=2), "expert", split_axis=0, concat_axis=0, tiled=True
    )
    taken = meta[:, :experts, :token_count] >= 0.0
    counts = jnp.sum(taken.astype(jnp.int32), axis=2)
    firsts = jnp.sum(taken[:, :, :half].astype(jnp.int32), axis=2)
    sums = jnp.sum(meta[:, :2, token_count:], axis=0)
    other = swapped(sums).reshape(2, chips, 2, local_count)[:, :, ::-1].reshape(2, all_experts)
    sums = sums + other
    tokens_all = token_count * 2 * chips
    loss = all_experts * jnp.sum(sums[0] / (tokens_all * top_count) * (sums[1] / tokens_all))

    x, z = place // SIDE, place % SIDE
    step = jnp.array(STEPS, jnp.int32)
    source = (((x + step) % SIDE)[:, None] * SIDE + ((z + step) % SIDE)[None, :]).reshape(-1)

    table = (counts, firsts, source, meta)
    near = expert_kernel(True, token_count, experts, cap, width, hidden)(*table, *a_near, *b_near, *own_w, *far_w)
    a_far, b_far, near = lax.optimization_barrier((a_far, b_far, near))
    rest = expert_kernel(False, token_count, experts, cap, width, hidden)(
        *table, *a_far, *b_far, *own_w, *far_w
    )

    def finish(near_out, far_out, first, second, lo):
        lines = reduce_line(*near_out, first).astype(jnp.bfloat16)
        far = reduce_line(*far_out, first).astype(jnp.bfloat16)
        own, low, high = (lines[i * half : (i + 1) * half] for i in range(3))
        cut = half // 2
        plus = jnp.concatenate([far[:cut], high[cut:]])
        minus = jnp.concatenate([far[cut:], low[:cut]])
        mixed = reduce_line(plus, minus, high[:cut], low[cut:], own, second)
        out = (inputs[lo : lo + half] + mixed).astype(jnp.bfloat16)
        count = lax.axis_size("section")
        return lax.ppermute(out, "section", [(s, (s + 1) % count) for s in range(count)])

    handed = jnp.concatenate(
        [
            finish(near[:5], rest[:5], along_x, along_z, 0),
            finish(near[5:], rest[5:], along_z, along_x, half),
        ]
    )
    return (handed[None], loss.reshape(1))


def solution(mesh):
    placed = (
        P("section", ("dp", "expert"), None),
        P("section", ("dp", "expert"), None),
        P("section", ("dp", "expert"), None),
        P("section", ("dp", "expert"), None, None),
        P("section", ("dp", "expert"), None, None),
        P("section", ("dp", "expert"), None, None),
    )
    return jax.shard_map(
        layer,
        mesh=mesh,
        in_specs=placed,
        out_specs=(P("section", ("dp", "expert"), None), P("section")),
        check_vma=False,
    )
```
